32 devices in a mesh: cuts: 2 (over x), mode: 8 (over z, y), branch: 2 (over core).
Axes of the slice: x: 2, y: 2, z: 4, core: 2. Of those that a mesh axis runs over, the one named last changes fastest.
Arguments:
- leaves: bfloat16 [8, 2, 32, 512, 512], P('branch', None, ('cuts', 'mode')), parts along dimension 2, may hold values from -0.1875 to 0.1875
- join_order: int32 [7], replicated, may hold values from 0 to 1
- slice_values: int32 [32], P(('cuts', 'mode')), parts along dimension 0, may hold values from 0 to 1
- boundary: bfloat16 [2, 2, 512, 512], replicated, may hold values from -4 to 4
Outputs:
- amplitudes: float32 [2, 32, 512, 512], P(None, ('cuts', 'mode'), 'branch'), parts along dimension 1
The draws below stay inside these ranges and needn't reach their ends.
There are 2 independent parts, one for each index of `cuts`. The reference program is written for one: setup_inputs(seed, part) draws one part's arguments, and reference() takes and returns one part's arrays. A program takes and returns all parts, laid end to end along the dimension named above; an argument that names none is the same for every part. Nothing has to cross between parts.
Inputs may be any that keep to these rules, and one draw needn't show every extreme that they name: `join_order`: 1 puts the second operand of the join on the left.
All inputs are finite; a program needn't handle non-finite values.
Results may differ from the reference program's by a relative error of at most 0.0076.
Values may be sent and summed in bfloat16 or wider, within the bound.
A program may use at most 64 MiB of HBM per device.

```python
import jax
import jax.numpy as jnp
from jax import lax

M = 512
LEAVES = 8
BOND = 2
BATCH = 16
N_MODE = 8


def with_ends(values, own_key, smallest, largest):
    extent = values.shape
    index_at = [jax.random.randint(jax.random.fold_in(own_key, axis), (), 0, extent[axis]) for axis in range(len(extent))]
    values = values.at[tuple(index_at)].set(smallest)
    longest = extent.index(max(extent))
    index_at[longest] = (index_at[longest] + 1) % extent[longest]
    return values.at[tuple(index_at)].set(largest)


def block_levels(own_key, extent, split, smallest, largest):
    def one(position, blocks):
        draws = jax.random.uniform(jax.random.fold_in(jax.random.fold_in(own_key, 6), position), (blocks,), jnp.float32, smallest / len(split), largest / len(split))
        return jnp.repeat(jnp.exp(draws), extent[position] // blocks).reshape((-1,) + (1,) * (len(extent) - position - 1))

    factor_of = one(*split[0])
    for cut in split[1:]:
        factor_of = factor_of * one(*cut)
    return factor_of


def bell_draw(own_key, shape, deviation, most, split=(), kind=jnp.bfloat16):
    array = deviation * jax.random.normal(own_key, shape, jnp.float32)
    if split:
        array = array * block_levels(own_key, shape, split, -0.22, 0.18)
    return jnp.clip(array, -most, most).astype(kind)


def setup_inputs(seed: int = 0, part: int = 0) -> dict:
    streams_of = jax.random.split(jax.random.key(seed), 5)
    own_keys = jax.random.split(jax.random.fold_in(streams_of[4], part), 5)
    leaves = bell_draw(own_keys[0], (LEAVES, 2, BATCH, M, M), (2 * M) ** -0.5, 0.1875, ((0, 2), (2, 8)))
    join_order = with_ends(jax.random.randint(streams_of[1], (LEAVES - 1,), 0, 2), jax.random.fold_in(streams_of[1], 1), 0, 1).astype(jnp.int32)
    slice_values = with_ends(jax.random.randint(own_keys[2], (BATCH,), 0, BOND), jax.random.fold_in(own_keys[2], 1), 0, BOND - 1).astype(jnp.int32)
    boundary = bell_draw(streams_of[3], (BOND, 2, M, M), 0.7, 4.0)
    return {"leaves": leaves, "join_order": join_order, "slice_values": slice_values, "boundary": boundary}


def complex_sums(left_op, right_op):
    spec = "bij,bjk->bik"
    left_real = left_op[0].astype(jnp.float32)
    left_imag = left_op[1].astype(jnp.float32)
    right_real = right_op[0].astype(jnp.float32)
    right_imag = right_op[1].astype(jnp.float32)
    real_part = jnp.einsum(spec, left_real, right_real) - jnp.einsum(spec, left_imag, right_imag)
    imag_part = jnp.einsum(spec, left_real, right_imag) + jnp.einsum(spec, left_imag, right_real)
    return jnp.stack([real_part, imag_part])


def complex_product(left_op, right_op):
    return complex_sums(left_op, right_op).astype(jnp.bfloat16)


def join_pair(left_op, right_op, swapped):
    return lax.cond(swapped == 1, lambda: complex_product(right_op, left_op), lambda: complex_product(left_op, right_op))


def reorder_rows(tensor):
    blocks = N_MODE
    block_rows = M // blocks
    viewed = tensor.reshape(2, BATCH, blocks, block_rows, M)
    return jnp.transpose(viewed, (0, 2, 1, 3, 4)).reshape(2, BATCH, M, M)


def reference(leaves, join_order, slice_values, boundary):
    first_level = []
    for index in range(4):
        joined = join_pair(leaves[2 * index], leaves[2 * index + 1], join_order[index])
        first_level.append(reorder_rows(joined))
    second_level = []
    for index in range(2):
        joined = join_pair(first_level[2 * index], first_level[2 * index + 1], join_order[4 + index])
        second_level.append(reorder_rows(joined))
    top_tensor = join_pair(second_level[0], second_level[1], join_order[6])
    chosen = jnp.where(slice_values[None, :, None, None] == 1, boundary[1][:, None], boundary[0][:, None])
    return complex_sums(top_tensor, chosen).astype(jnp.float32)
```

```python
import functools

import jax
import jax.numpy as jnp
from jax import lax
from jax.experimental import pallas as pl
from jax.experimental.pallas import tpu as pltpu
from jax.sharding import PartitionSpec as P

MESH = pl.DeviceIdType.MESH


def dot(left, right):
    return jnp.dot(left, right, preferred_element_type=jnp.float32)


def complex_rows(left_real, left_imag, right_real, right_imag):
    real_part = dot(left_real, right_real) - dot(left_imag, right_imag)
    imag_part = dot(left_real, right_imag) + dot(left_imag, right_real)
    return real_part, imag_part


def join_kernel(tile, order_ref, left_ref, right_ref, out_ref):
    rows = left_ref.shape[-2]

    @pl.loop(0, rows // tile)
    def _(step):
        at = pl.ds(pl.multiple_of(step * tile, tile), tile)
        real_part, imag_part = complex_rows(
            left_ref[0, 0, 0, at, :],
            left_ref[0, 1, 0, at, :],
            right_ref[0, 0, 0],
            right_ref[0, 1, 0],
        )
        out_ref[0, 0, 0, at, :] = real_part.astype(out_ref.dtype)
        out_ref[0, 1, 0, at, :] = imag_part.astype(out_ref.dtype)


def first_joins(leaves, order):
    _, _, per, m, width = leaves.shape
    block = (1, 2, 1, m, width)
    return pl.pallas_call(
        functools.partial(join_kernel, min(256, m)),
        out_shape=jax.ShapeDtypeStruct((2, 2, per, m, width), leaves.dtype),
        grid_spec=pltpu.PrefetchScalarGridSpec(
            num_scalar_prefetch=1,
            grid=(2, per),
            in_specs=[
                pl.BlockSpec(block, lambda k, e, order: (order[2 * k], 0, e, 0, 0)),
                pl.BlockSpec(block, lambda k, e, order: (order[2 * k + 1], 0, e, 0, 0)),
            ],
            out_specs=pl.BlockSpec(block, lambda k, e, order: (k, 0, e, 0, 0)),
        ),
        name="first_joins",
    )(order, leaves, leaves)


def middle_kernel(
    n, per, prod_ref, out_ref, gathered, result,
    send1, recv1, local1, send3, recv3, local3, sendf, recvf,
):
    group = n // per
    m = lax.axis_index("mode")
    core = lax.axis_index("branch")
    h, g = m // group, m % group
    blk, width = prod_ref.shape[-2:]

    def regroup_copy(t, slot, k):
        to = lax.rem(g + k, group)
        return pltpu.make_async_remote_copy(
            src_ref=prod_ref.at[slot, :, :, per * to + t],
            dst_ref=gathered.at[t, slot, :, pl.ds(per * g, per)],
            send_sem=send1.at[t, slot, k],
            recv_sem=recv1.at[t, slot, k],
            device_id={"mode": h * group + to},
            device_id_type=MESH,
        )

    def regroup_arrival(t, slot, k):
        source = lax.rem(g + group - k, group)
        return pltpu.make_async_remote_copy(
            src_ref=prod_ref.at[slot, :, :, per * g + t],
            dst_ref=gathered.at[t, slot, :, pl.ds(per * source, per)],
            send_sem=send1.at[t, slot, k],
            recv_sem=recv1.at[t, slot, k],
            device_id={"mode": h * group + source},
            device_id_type=MESH,
        )

    def own_copy(t, slot):
        return pltpu.make_async_copy(
            prod_ref.at[slot, :, :, per * g + t],
            gathered.at[t, slot, :, pl.ds(per * g, per)],
            local1.at[t, slot],
        )

    def place(source, t):
        batch = per * (per * lax.rem(source, group) + t) + source // group
        return batch // n, lax.rem(batch, n)

    def deliver_copy(t, k):
        to = lax.rem(m + k, n)
        entry, row = place(m, t)
        return pltpu.make_async_remote_copy(
            src_ref=result.at[t, :, to],
            dst_ref=out_ref.at[core, entry, :, row],
            send_sem=send3.at[t, k],
            recv_sem=recv3.at[t, k],
            device_id={"mode": to},
            device_id_type=MESH,
        )

    def deliver_arrival(t, k):
        source = lax.rem(m + n - k, n)
        entry, row = place(source, t)
        return pltpu.make_async_remote_copy(
            src_ref=result.at[t, :, source],
            dst_ref=out_ref.at[core, entry, :, row],
            send_sem=send3.at[t, k],
            recv_sem=recv3.at[t, k],
            device_id={"mode": source},
            device_id_type=MESH,
        )

    def own_deliver(t):
        entry, row = place(m, t)
        return pltpu.make_async_copy(
            result.at[t, :, m], out_ref.at[core, entry, :, row], local3.at[t]
        )

    def forward_copy(t, k, owner):
        source = lax.rem(m + n - k, n)
        entry, row = place(source, t)
        part = out_ref.at[owner, entry, :, row]
        return pltpu.make_async_remote_copy(
            src_ref=part,
            dst_ref=part,
            send_sem=sendf.at[t, k],
            recv_sem=recvf.at[t, k],
            device_id={"branch": 1 - core},
            device_id_type=MESH,
        )

    barrier = pltpu.get_barrier_semaphore()
    for k in range(1, n):
        pl.semaphore_signal(
            barrier, inc=1, device_id={"mode": lax.rem(m + k, n)}, device_id_type=MESH
        )
    pl.semaphore_signal(barrier, inc=1, device_id={"branch": 1 - core}, device_id_type=MESH)
    pl.semaphore_wait(barrier, n)

    for t in range(per):
        for slot in range(2):
            for k in range(1, group):
                regroup_copy(t, slot, k).start()
            own_copy(t, slot).start()

    tile_blocks = max(1, min(n, 256 // blk))
    tile = tile_blocks * blk
    for t in range(per):
        for slot in range(2):
            own_copy(t, slot).wait()
            for k in range(1, group):
                regroup_arrival(t, slot, k).wait_recv()

        @pl.loop(0, n // tile_blocks)
        def _(step):
            at = pl.ds(step * tile_blocks, tile_blocks)
            real_part, imag_part = complex_rows(
                gathered[t, 1, 0, at].reshape(tile, width),
                gathered[t, 1, 1, at].reshape(tile, width),
                gathered[t, 0, 0].reshape(n * blk, width),
                gathered[t, 0, 1].reshape(n * blk, width),
            )
            shape = (tile_blocks, blk, width)
            result[t, 0, at] = real_part.astype(result.dtype).reshape(shape)
            result[t, 1, at] = imag_part.astype(result.dtype).reshape(shape)

        for k in range(1, n):
            deliver_copy(t, k).start()
        own_deliver(t).start()

    for t in range(per):
        own_deliver(t).wait()
        forward_copy(t, 0, core).start()
        for k in range(1, n):
            deliver_arrival(t, k).wait_recv()
            forward_copy(t, k, core).start()

    for t in range(per):
        for slot in range(2):
            for k in range(1, group):
                regroup_copy(t, slot, k).wait_send()
        for k in range(1, n):
            deliver_copy(t, k).wait_send()
        for k in range(n):
            forward_copy(t, k, core).wait_send()
            forward_copy(t, k, 1 - core).wait_recv()


def middle_join(products, n, per):
    _, _, _, _, blk, width = products.shape
    group = n // per
    dma = pltpu.SemaphoreType.DMA
    return pl.pallas_call(
        functools.partial(middle_kernel, n, per),
        out_shape=jax.ShapeDtypeStruct((2, per, 2, n, blk, width), products.dtype),
        in_specs=[pl.BlockSpec(memory_space=pl.ANY)],
        out_specs=pl.BlockSpec(memory_space=pl.ANY),
        scratch_shapes=[
            pltpu.VMEM((per, 2, 2, n, blk, width), products.dtype),
            pltpu.VMEM((per, 2, n, blk, width), products.dtype),
            dma((per, 2, group)),
            dma((per, 2, group)),
            dma((per, 2)),
            dma((per, n)),
            dma((per, n)),
            dma((per,)),
            dma((per, n)),
            dma((per, n)),
        ],
        compiler_params=pltpu.CompilerParams(collective_id=0, has_side_effects=True),
        name="middle_join",
    )(products)


def top_kernel(picks_ref, left_ref, right_ref, chosen_ref, out_ref):
    top_real, top_imag = complex_rows(
        left_ref[0, 0, 0], left_ref[0, 0, 1], right_ref[0, 0, 0], right_ref[0, 0, 1]
    )
    dtype = left_ref.dtype
    real_part, imag_part = complex_rows(
        top_real.astype(dtype), top_imag.astype(dtype), chosen_ref[0, 0], chosen_ref[0, 1]
    )
    out_ref[0, 0] = real_part
    out_ref[1, 0] = imag_part


def top_join(middles, boundary, picks, per):
    m, width = boundary.shape[-2:]
    half = m // 2
    return pl.pallas_call(
        top_kernel,
        out_shape=jax.ShapeDtypeStruct((2, per, half, width), jnp.float32),
        grid_spec=pltpu.PrefetchScalarGridSpec(
            num_scalar_prefetch=1,
            grid=(per,),
            in_specs=[
                pl.BlockSpec((1, 1, 2, half, width), lambda e, p: (p[0], e, 0, p[1], 0)),
                pl.BlockSpec((1, 1, 2, m, width), lambda e, p: (1 - p[0], e, 0, 0, 0)),
                pl.BlockSpec((1, 2, m, width), lambda e, p: (p[2 + e], 0, 0, 0)),
            ],
            out_specs=pl.BlockSpec((2, 1, half, width), lambda e, p: (0, e, 0, 0)),
        ),
        name="top_join",
    )(picks, middles, middles, boundary)


def per_device(leaves, join_order, slice_values, boundary):
    n = lax.axis_size("mode")
    core = lax.axis_index("branch")
    _, _, per, m, width = leaves.shape
    order = join_order.astype(jnp.int32)
    own = lax.dynamic_slice_in_dim(order, 2 * core, 2)
    middle_order = lax.dynamic_slice_in_dim(order, 4 + core, 1)[0]
    right_pair = 1 - middle_order
    left_pair = middle_order
    right_flag = jnp.where(right_pair == 1, own[1], own[0])
    left_flag = jnp.where(left_pair == 1, own[1], own[0])
    leaf_order = jnp.stack(
        [
            2 * right_pair + right_flag,
            2 * right_pair + 1 - right_flag,
            2 * left_pair + left_flag,
            2 * left_pair + 1 - left_flag,
        ]
    )
    products = first_joins(leaves, leaf_order)
    products = products.reshape(2, 2, per, n, m // n, width)
    middles = middle_join(products, n, per).reshape(2, per, 2, m, width)
    picks = jnp.concatenate([order[6:7], core[None].astype(jnp.int32), slice_values])
    return top_join(middles, boundary, picks, per)


def solution(mesh):
    in_specs = (P("branch", None, ("cuts", "mode"), None, None), P(), P(("cuts", "mode")), P())
    out_specs = P(None, ("cuts", "mode"), "branch", None)
    return jax.shard_map(
        per_device, mesh=mesh, in_specs=in_specs, out_specs=out_specs, check_vma=False
    )
```

```python
import functools

import jax
import jax.numpy as jnp
from jax import lax
from jax.experimental import pallas as pl
from jax.experimental.pallas import tpu as pltpu
from jax.sharding import PartitionSpec as P

MESH = pl.DeviceIdType.MESH


def dot(left, right):
    return jnp.dot(left, right, preferred_element_type=jnp.float32)


def complex_rows(left_real, left_imag, right_real, right_imag):
    real_part = dot(left_real, right_real) - dot(left_imag, right_imag)
    imag_part = dot(left_real, right_imag) + dot(left_imag, right_real)
    return real_part, imag_part


def contract_kernel(
    per, order_ref, leaves_ref, out_ref, prod, right, left, result,
    leaf_sem, own_right, own_left,
    cross_right_send, cross_right_recv, cross_left_send, cross_left_recv,
    column_send, column_recv, relay_send, relay_recv,
    deliver_send, deliver_recv, forward_send, forward_recv, *leaf,
):
    n = lax.axis_size("mode")
    group = n // per
    pair = 2
    peers = group // pair
    rounds = n // pair
    wide = pair * per
    m = lax.axis_index("mode")
    core = lax.axis_index("branch")
    h, g = m // group, lax.rem(m, group)
    line, side = g // pair, lax.rem(g, pair)
    across = pair * line + 1 - side
    blk, width = out_ref.shape[-2:]
    order = n * blk

    def remote(src, dst, send, recv, **device):
        return pltpu.make_async_remote_copy(
            src_ref=src,
            dst_ref=dst,
            send_sem=send,
            recv_sem=recv,
            device_id=device,
            device_id_type=MESH,
        )

    def column(line_at):
        return pair * line_at + side

    def up(k):
        return lax.rem(line + k, peers)

    def down(k):
        return lax.rem(line + peers - k, peers)

    def own_right_copy(q, e):
        return pltpu.make_async_copy(
            prod.at[0, :, e, pair * q + side], right.at[q, :, per * g + e], own_right.at[q, e]
        )

    def own_left_copy(q, e):
        return pltpu.make_async_copy(
            prod.at[1, :, e, pair * q + side], left.at[q, :, per * side + e], own_left.at[q, e]
        )

    def cross_right(q, e, source=None):
        return remote(
            prod.at[0, :, e, pair * q + 1 - side],
            right.at[q, :, per * (g if source is None else source) + e],
            cross_right_send.at[q, e],
            cross_right_recv.at[q, e],
            mode=h * group + across,
        )

    def cross_left(q, e, source=None):
        return remote(
            prod.at[1, :, e, pair * q + 1 - side],
            left.at[q, :, per * (side if source is None else source) + e],
            cross_left_send.at[q, e],
            cross_left_recv.at[q, e],
            mode=h * group + across,
        )

    def column_right(q, e, k, target, source):
        return remote(
            prod.at[0, :, e, pair * q + side],
            right.at[q, :, per * column(source) + e],
            column_send.at[q, e, k],
            column_recv.at[q, e, k],
            mode=h * group + column(target),
        )

    def relay_right(q, e, k, target, source):
        part = right.at[q, :, per * (pair * source + 1 - side) + e]
        return remote(
            part,
            part,
            relay_send.at[q, e, k],
            relay_recv.at[q, e, k],
            mode=h * group + column(target),
        )

    def spot(q, h_from, side_from):
        batch = per * (pair * q + side_from) + h_from
        return batch // n, lax.rem(batch, n)

    def deliver(q, i):
        entry, row = spot(q, h, side)
        at = pair * h + side
        return remote(
            result.at[q, :, i],
            out_ref.at[core, entry, :, row],
            deliver_send.at[q, i],
            deliver_recv.at[q, at],
            mode=wide * line + i,
        )

    def deliver_own(q, i):
        entry, row = spot(q, h, side)
        return pltpu.make_async_copy(
            result.at[q, :, i],
            out_ref.at[core, entry, :, row],
            deliver_recv.at[q, pair * h + side],
        )

    def delivered(q, h_from, side_from):
        entry, row = spot(q, h_from, side_from)
        part = out_ref.at[core, entry, :, row]
        return pltpu.make_async_copy(part, part, deliver_recv.at[q, pair * h_from + side_from])

    def forward(q, h_from, side_from, owner):
        entry, row = spot(q, h_from, side_from)
        part = out_ref.at[owner, entry, :, row]
        at = pair * h_from + side_from
        return remote(
            part, part, forward_send.at[q, at], forward_recv.at[q, at], branch=1 - core
        )

    def leaf_copy(e):
        return pltpu.make_async_copy(leaves_ref.at[:, :, e], leaf[e], leaf_sem.at[e])

    middle_order = order_ref[4 + core]
    tile = min(256, order)

    def first_join(slot, e):
        which = 1 - middle_order if slot == 0 else middle_order
        flag = order_ref[2 * core + which]
        left_leaf = 2 * which + flag
        right_leaf = 2 * which + 1 - flag

        @pl.loop(0, order // tile)
        def _(step):
            at = pl.ds(pl.multiple_of(step * tile, tile), tile)
            real_part, imag_part = complex_rows(
                leaf[e][left_leaf, 0, at, :],
                leaf[e][left_leaf, 1, at, :],
                leaf[e][right_leaf, 0],
                leaf[e][right_leaf, 1],
            )
            blocks = tile // blk
            shape = (blocks, blk, width)
            to = pl.ds(step * blocks, blocks)
            prod[slot, 0, e, to] = real_part.astype(prod.dtype).reshape(shape)
            prod[slot, 1, e, to] = imag_part.astype(prod.dtype).reshape(shape)

    def send_cross_right(q, e):
        cross_right(q, e).start()

    def send_column(q, e):
        for k in range(1, peers):
            column_right(q, e, k, up(k), line).start()
        own_right_copy(q, e).start()

    def send_cross_left(q, e):
        cross_left(q, e).start()
        own_left_copy(q, e).start()

    def send_relay(q, e):
        cross_right(q, e, across).wait_recv()
        for k in range(1, peers):
            relay_right(q, e, k, up(k), line).start()

    barrier = pltpu.get_barrier_semaphore()
    for k in range(1, n):
        pl.semaphore_signal(
            barrier, inc=1, device_id={"mode": lax.rem(m + k, n)}, device_id_type=MESH
        )
    pl.semaphore_signal(barrier, inc=1, device_id={"branch": 1 - core}, device_id_type=MESH)
    for e in range(per):
        leaf_copy(e).start()

    for e in range(per):
        leaf_copy(e).wait()
        first_join(0, e)
        if e == 0:
            pl.semaphore_wait(barrier, n)
        send_cross_right(0, e)
        send_column(0, e)
    for e in range(per):
        first_join(1, e)
        send_cross_left(0, e)
        send_relay(0, e)
    for q in range(1, rounds):
        for e in range(per):
            send_cross_right(q, e)
        for e in range(per):
            send_cross_left(q, e)

    row_tile = wide * blk
    for q in range(rounds):
        if q + 1 < rounds:
            for e in range(per):
                send_column(q + 1, e)
        for e in range(per):
            own_right_copy(q, e).wait()
            own_left_copy(q, e).wait()
            cross_left(q, e, 1 - side).wait_recv()
            for k in range(1, peers):
                column_right(q, e, k, down(k), down(k)).wait_recv()
                relay_right(q, e, k, down(k), down(k)).wait_recv()

        real_part, imag_part = complex_rows(
            left[q, 0].reshape(row_tile, width),
            left[q, 1].reshape(row_tile, width),
            right[q, 0].reshape(order, width),
            right[q, 1].reshape(order, width),
        )
        result[q, 0] = real_part.astype(result.dtype).reshape(wide, blk, width)
        result[q, 1] = imag_part.astype(result.dtype).reshape(wide, blk, width)

        for i in range(wide):
            here = wide * line + i == m

            @pl.when(jnp.logical_not(here))
            def _():
                deliver(q, i).start()

            @pl.when(here)
            def _():
                deliver_own(q, i).start()

        if q + 1 < rounds:
            for e in range(per):
                send_relay(q + 1, e)

    for q in range(rounds):
        for h_from in range(per):
            for side_from in range(pair):
                delivered(q, h_from, side_from).wait()
                forward(q, h_from, side_from, core).start()

    for q in range(rounds):
        for e in range(per):
            cross_right(q, e).wait_send()
            cross_left(q, e).wait_send()
            for k in range(1, peers):
                column_right(q, e, k, up(k), line).wait_send()
                relay_right(q, e, k, up(k), line).wait_send()
        for i in range(wide):

            @pl.when(wide * line + i != m)
            def _():
                deliver(q, i).wait_send()

        for h_from in range(per):
            for side_from in range(pair):
                forward(q, h_from, side_from, core).wait_send()
                forward(q, h_from, side_from, 1 - core).wait_recv()


def lower_levels(leaves, join_order):
    n = lax.axis_size("mode")
    count, _, per, order, width = leaves.shape
    blk = order // n
    rounds, peers, wide = n // 2, n // per // 2, 2 * per
    dma = pltpu.SemaphoreType.DMA
    dtype = leaves.dtype
    return pl.pallas_call(
        functools.partial(contract_kernel, per),
        out_shape=jax.ShapeDtypeStruct((2, per, 2, n, blk, width), dtype),
        in_specs=[
            pl.BlockSpec(memory_space=pltpu.SMEM),
            pl.BlockSpec(memory_space=pl.ANY),
        ],
        out_specs=pl.BlockSpec(memory_space=pl.ANY),
        scratch_shapes=[
            pltpu.VMEM((2, 2, per, n, blk, width), dtype),
            pltpu.VMEM((rounds, 2, n, blk, width), dtype),
            pltpu.VMEM((rounds, 2, wide, blk, width), dtype),
            pltpu.VMEM((rounds, 2, wide, blk, width), dtype),
            dma((per,)),
            dma((rounds, per)),
            dma((rounds, per)),
            dma((rounds, per)),
            dma((rounds, per)),
            dma((rounds, per)),
            dma((rounds, per)),
            dma((rounds, per, peers)),
            dma((rounds, per, peers)),
            dma((rounds, per, peers)),
            dma((rounds, per, peers)),
            dma((rounds, wide)),
            dma((rounds, wide)),
            dma((rounds, wide)),
            dma((rounds, wide)),
        ]
        + [pltpu.VMEM((count, 2, order, width), dtype)] * per,
        compiler_params=pltpu.CompilerParams(collective_id=0, has_side_effects=True),
        name="lower_levels",
    )(join_order, leaves)


def top_kernel(order_ref, slices_ref, left_ref, right_ref, chosen_ref, out_ref):
    half = out_ref.shape[-2]
    at = pl.ds(pl.multiple_of(lax.axis_index("branch") * half, half), half)
    top_real, top_imag = complex_rows(
        left_ref[0, 0, 0, at, :], left_ref[0, 0, 1, at, :], right_ref[0, 0, 0], right_ref[0, 0, 1]
    )
    dtype = left_ref.dtype
    real_part, imag_part = complex_rows(
        top_real.astype(dtype), top_imag.astype(dtype), chosen_ref[0, 0], chosen_ref[0, 1]
    )
    out_ref[0, 0] = real_part
    out_ref[1, 0] = imag_part


def top_join(middles, boundary, join_order, slice_values, per):
    order, width = boundary.shape[-2:]
    half = order // 2
    last = join_order.shape[0] - 1
    return pl.pallas_call(
        top_kernel,
        out_shape=jax.ShapeDtypeStruct((2, per, half, width), jnp.float32),
        grid_spec=pltpu.PrefetchScalarGridSpec(
            num_scalar_prefetch=2,
            grid=(per,),
            in_specs=[
                pl.BlockSpec((1, 1, 2, order, width), lambda e, o, s: (o[last], e, 0, 0, 0)),
                pl.BlockSpec((1, 1, 2, order, width), lambda e, o, s: (1 - o[last], e, 0, 0, 0)),
                pl.BlockSpec((1, 2, order, width), lambda e, o, s: (s[e], 0, 0, 0)),
            ],
            out_specs=pl.BlockSpec((2, 1, half, width), lambda e, o, s: (0, e, 0, 0)),
        ),
        name="top_join",
    )(join_order, slice_values, middles, middles, boundary)


def per_device(leaves, join_order, slice_values, boundary):
    _, _, per, order, width = leaves.shape
    middles = lower_levels(leaves, join_order).reshape(2, per, 2, order, width)
    return top_join(middles, boundary, join_order, slice_values, per)


def solution(mesh):
    in_specs = (P("branch", None, ("cuts", "mode"), None, None), P(), P(("cuts", "mode")), P())
    out_specs = P(None, ("cuts", "mode"), "branch", None)
    return jax.shard_map(
        per_device, mesh=mesh, in_specs=in_specs, out_specs=out_specs, check_vma=False
    )
```

```python
import functools

import jax
import jax.numpy as jnp
from jax import lax
from jax.experimental import pallas as pl
from jax.experimental.pallas import tpu as pltpu
from jax.sharding import PartitionSpec as P

MESH = pl.DeviceIdType.MESH


def dot(left, right):
    return jnp.dot(left, right, preferred_element_type=jnp.float32)


def complex_rows(left_real, left_imag, right_real, right_imag):
    real_part = dot(left_real, right_real) - dot(left_imag, right_imag)
    imag_part = dot(left_real, right_imag) + dot(left_imag, right_real)
    return real_part, imag_part


def contract_kernel(
    per, order_ref, leaves_ref, out_ref, prod, right, left, result,
    leaf_sem, own_right, own_left,
    cross_right_send, cross_right_recv, cross_left_send, cross_left_recv,
    column_send, column_recv, relay_send, relay_recv,
    deliver_send, deliver_recv, forward_send, forward_recv, *leaf,
):
    n = lax.axis_size("mode")
    group = n // per
    pair = 2
    peers = group // pair
    rounds = n // pair
    wide = pair * per
    m = lax.axis_index("mode")
    core = lax.axis_index("branch")
    h, g = m // group, lax.rem(m, group)
    line, side = g // pair, lax.rem(g, pair)
    across = pair * line + 1 - side
    blk, width = out_ref.shape[-2:]
    order = n * blk

    def remote(src, dst, send, recv, **device):
        return pltpu.make_async_remote_copy(
            src_ref=src,
            dst_ref=dst,
            send_sem=send,
            recv_sem=recv,
            device_id=device,
            device_id_type=MESH,
        )

    def column(line_at):
        return pair * line_at + side

    def up(k):
        return lax.rem(line + k, peers)

    def down(k):
        return lax.rem(line + peers - k, peers)

    def own_right_copy(q, e):
        return pltpu.make_async_copy(
            prod.at[0, :, e, pair * q + side], right.at[q, :, per * g + e], own_right.at[q, e]
        )

    def own_left_copy(q, e):
        return pltpu.make_async_copy(
            prod.at[1, :, e, pair * q + side], left.at[q, :, per * side + e], own_left.at[q, e]
        )

    def cross_right(q, e, source=None):
        return remote(
            prod.at[0, :, e, pair * q + 1 - side],
            right.at[q, :, per * (g if source is None else source) + e],
            cross_right_send.at[q, e],
            cross_right_recv.at[q, e],
            mode=h * group + across,
        )

    def cross_left(q, e, source=None):
        return remote(
            prod.at[1, :, e, pair * q + 1 - side],
            left.at[q, :, per * (side if source is None else source) + e],
            cross_left_send.at[q, e],
            cross_left_recv.at[q, e],
            mode=h * group + across,
        )

    def column_right(q, e, k, target, source):
        return remote(
            prod.at[0, :, e, pair * q + side],
            right.at[q, :, per * column(source) + e],
            column_send.at[q, e, k],
            column_recv.at[q, e, k],
            mode=h * group + column(target),
        )

    def relay_right(q, e, k, target, source):
        part = right.at[q, :, per * (pair * source + 1 - side) + e]
        return remote(
            part,
            part,
            relay_send.at[q, e, k],
            relay_recv.at[q, e, k],
            mode=h * group + column(target),
        )

    def spot(q, h_from, side_from):
        batch = per * (pair * q + side_from) + h_from
        return batch // n, lax.rem(batch, n)

    def deliver(q, i):
        entry, row = spot(q, h, side)
        at = pair * h + side
        return remote(
            result.at[q, :, i],
            out_ref.at[core, entry, :, row],
            deliver_send.at[q, i],
            deliver_recv.at[q, at],
            mode=wide * line + i,
        )

    def deliver_own(q, i):
        entry, row = spot(q, h, side)
        return pltpu.make_async_copy(
            result.at[q, :, i],
            out_ref.at[core, entry, :, row],
            deliver_recv.at[q, pair * h + side],
        )

    def delivered(q, h_from, side_from):
        entry, row = spot(q, h_from, side_from)
        part = out_ref.at[core, entry, :, row]
        return pltpu.make_async_copy(part, part, deliver_recv.at[q, pair * h_from + side_from])

    def forward(q, h_from, side_from, owner):
        entry, row = spot(q, h_from, side_from)
        part = out_ref.at[owner, entry, :, row]
        at = pair * h_from + side_from
        return remote(
            part, part, forward_send.at[q, at], forward_recv.at[q, at], branch=1 - core
        )

    def leaf_copy(e):
        return pltpu.make_async_copy(leaves_ref.at[:, :, e], leaf[e], leaf_sem.at[e])

    middle_order = order_ref[4 + core]
    tile = min(256, order)

    def first_join(slot, e):
        which = 1 - middle_order if slot == 0 else middle_order
        flag = order_ref[2 * core + which]
        left_leaf = 2 * which + flag
        right_leaf = 2 * which + 1 - flag

        @pl.loop(0, order // tile)
        def _(step):
            at = pl.ds(pl.multiple_of(step * tile, tile), tile)
            real_part, imag_part = complex_rows(
                leaf[e][left_leaf, 0, at, :],
                leaf[e][left_leaf, 1, at, :],
                leaf[e][right_leaf, 0],
                leaf[e][right_leaf, 1],
            )
            blocks = tile // blk
            shape = (blocks, blk, width)
            to = pl.ds(step * blocks, blocks)
            prod[slot, 0, e, to] = real_part.astype(prod.dtype).reshape(shape)
            prod[slot, 1, e, to] = imag_part.astype(prod.dtype).reshape(shape)

    def send_cross_right(q, e):
        cross_right(q, e).start()

    def send_column(q, e):
        for k in range(1, peers):
            column_right(q, e, k, up(k), line).start()
        own_right_copy(q, e).start()

    def send_cross_left(q, e):
        cross_left(q, e).start()
        own_left_copy(q, e).start()

    def send_relay(q, e):
        cross_right(q, e, across).wait_recv()
        for k in range(1, peers):
            relay_right(q, e, k, up(k), line).start()

    barrier = pltpu.get_barrier_semaphore()
    for k in range(1, n):
        pl.semaphore_signal(
            barrier, inc=1, device_id={"mode": lax.rem(m + k, n)}, device_id_type=MESH
        )
    pl.semaphore_signal(barrier, inc=1, device_id={"branch": 1 - core}, device_id_type=MESH)
    for e in range(per):
        leaf_copy(e).start()

    for e in range(per):
        leaf_copy(e).wait()
        first_join(0, e)
        if e == 0:
            pl.semaphore_wait(barrier, n)
        send_cross_right(0, e)
        send_column(0, e)
    ahead = min(2, rounds)
    for q in range(1, ahead):
        for e in range(per):
            send_cross_right(q, e)
            send_column(q, e)
    for e in range(per):
        first_join(1, e)
        send_cross_left(0, e)
    for q in range(ahead, rounds):
        for e in range(per):
            send_cross_right(q, e)
        for e in range(per):
            send_cross_left(q - 1, e)
    for q in range(max(1, rounds - 1), rounds):
        for e in range(per):
            send_cross_left(q, e)
    for q in range(ahead):
        for e in range(per):
            send_relay(q, e)
    for q in range(ahead, min(ahead + 1, rounds)):
        for e in range(per):
            send_column(q, e)

    def send_results(q, late):
        for i in range(wide):
            target = wide * line + i
            same_group = target // group == h
            same_line = lax.rem(target, group) // pair == line
            waits = jnp.logical_and(same_group, jnp.logical_not(same_line))
            if late:

                @pl.when(waits)
                def _():
                    deliver(q, i).start()

            else:

                @pl.when(jnp.logical_not(jnp.logical_or(waits, target == m)))
                def _():
                    deliver(q, i).start()

                @pl.when(target == m)
                def _():
                    deliver_own(q, i).start()

    row_tile = wide * blk
    held = []
    for q in range(rounds):
        for e in range(per):
            own_right_copy(q, e).wait()
            own_left_copy(q, e).wait()
            cross_left(q, e, 1 - side).wait_recv()
            for k in range(1, peers):
                column_right(q, e, k, down(k), down(k)).wait_recv()
                relay_right(q, e, k, down(k), down(k)).wait_recv()

        real_part, imag_part = complex_rows(
            left[q, 0].reshape(row_tile, width),
            left[q, 1].reshape(row_tile, width),
            right[q, 0].reshape(order, width),
            right[q, 1].reshape(order, width),
        )
        result[q, 0] = real_part.astype(result.dtype).reshape(wide, blk, width)
        result[q, 1] = imag_part.astype(result.dtype).reshape(wide, blk, width)

        send_results(q, False)
        held.append(q)
        for later in range(q + ahead, min(q + ahead + 1, rounds)):
            for e in range(per):
                send_relay(later, e)
        for later in range(q + ahead + 1, min(q + ahead + 2, rounds)):
            for e in range(per):
                send_column(later, e)
        if q + ahead + 1 >= rounds:
            for earlier in held:
                send_results(earlier, True)
            held = []

    for q in range(rounds):
        for h_from in range(per):
            for side_from in range(pair):
                delivered(q, h_from, side_from).wait()
                forward(q, h_from, side_from, core).start()

    for q in range(rounds):
        for e in range(per):
            cross_right(q, e).wait_send()
            cross_left(q, e).wait_send()
            for k in range(1, peers):
                column_right(q, e, k, up(k), line).wait_send()
                relay_right(q, e, k, up(k), line).wait_send()
        for i in range(wide):

            @pl.when(wide * line + i != m)
            def _():
                deliver(q, i).wait_send()

        for h_from in range(per):
            for side_from in range(pair):
                forward(q, h_from, side_from, core).wait_send()
                forward(q, h_from, side_from, 1 - core).wait_recv()


def lower_levels(leaves, join_order):
    n = lax.axis_size("mode")
    count, _, per, order, width = leaves.shape
    blk = order // n
    rounds, peers, wide = n // 2, n // per // 2, 2 * per
    dma = pltpu.SemaphoreType.DMA
    dtype = leaves.dtype
    return pl.pallas_call(
        functools.partial(contract_kernel, per),
        out_shape=jax.ShapeDtypeStruct((2, per, 2, n, blk, width), dtype),
        in_specs=[
            pl.BlockSpec(memory_space=pltpu.SMEM),
            pl.BlockSpec(memory_space=pl.ANY),
        ],
        out_specs=pl.BlockSpec(memory_space=pl.ANY),
        scratch_shapes=[
            pltpu.VMEM((2, 2, per, n, blk, width), dtype),
            pltpu.VMEM((rounds, 2, n, blk, width), dtype),
            pltpu.VMEM((rounds, 2, wide, blk, width), dtype),
            pltpu.VMEM((rounds, 2, wide, blk, width), dtype),
            dma((per,)),
            dma((rounds, per)),
            dma((rounds, per)),
            dma((rounds, per)),
            dma((rounds, per)),
            dma((rounds, per)),
            dma((rounds, per)),
            dma((rounds, per, peers)),
            dma((rounds, per, peers)),
            dma((rounds, per, peers)),
            dma((rounds, per, peers)),
            dma((rounds, wide)),
            dma((rounds, wide)),
            dma((rounds, wide)),
            dma((rounds, wide)),
        ]
        + [pltpu.VMEM((count, 2, order, width), dtype)] * per,
        compiler_params=pltpu.CompilerParams(collective_id=0, has_side_effects=True),
        name="lower_levels",
    )(join_order, leaves)


def top_kernel(order_ref, slices_ref, left_ref, right_ref, chosen_ref, out_ref):
    half = out_ref.shape[-2]
    at = pl.ds(pl.multiple_of(lax.axis_index("branch") * half, half), half)
    top_real, top_imag = complex_rows(
        left_ref[0, 0, 0, at, :], left_ref[0, 0, 1, at, :], right_ref[0, 0, 0], right_ref[0, 0, 1]
    )
    dtype = left_ref.dtype
    real_part, imag_part = complex_rows(
        top_real.astype(dtype), top_imag.astype(dtype), chosen_ref[0, 0], chosen_ref[0, 1]
    )
    out_ref[0, 0] = real_part
    out_ref[1, 0] = imag_part


def top_join(middles, boundary, join_order, slice_values, per):
    order, width = boundary.shape[-2:]
    half = order // 2
    last = join_order.shape[0] - 1
    return pl.pallas_call(
        top_kernel,
        out_shape=jax.ShapeDtypeStruct((2, per, half, width), jnp.float32),
        grid_spec=pltpu.PrefetchScalarGridSpec(
            num_scalar_prefetch=2,
            grid=(per,),
            in_specs=[
                pl.BlockSpec((1, 1, 2, order, width), lambda e, o, s: (o[last], e, 0, 0, 0)),
                pl.BlockSpec((1, 1, 2, order, width), lambda e, o, s: (1 - o[last], e, 0, 0, 0)),
                pl.BlockSpec((1, 2, order, width), lambda e, o, s: (s[e], 0, 0, 0)),
            ],
            out_specs=pl.BlockSpec((2, 1, half, width), lambda e, o, s: (0, e, 0, 0)),
        ),
        name="top_join",
    )(join_order, slice_values, middles, middles, boundary)


def per_device(leaves, join_order, slice_values, boundary):
    _, _, per, order, width = leaves.shape
    middles = lower_levels(leaves, join_order).reshape(2, per, 2, order, width)
    return top_join(middles, boundary, join_order, slice_values, per)


def solution(mesh):
    in_specs = (P("branch", None, ("cuts", "mode"), None, None), P(), P(("cuts", "mode")), P())
    out_specs = P(None, ("cuts", "mode"), "branch", None)
    return jax.shard_map(
        per_device, mesh=mesh, in_specs=in_specs, out_specs=out_specs, check_vma=False
    )
```
